32 devices in a mesh: dp: 8 (over y, x, core), mp: 4 (over z).
Axes of the slice: x: 2, y: 2, z: 4, core: 2. Of those that a mesh axis runs over, the one named last changes fastest.
Arguments:
- embeddings: bfloat16 [65536, 2560], P('dp', 'mp')
- centroids: bfloat16 [16384, 2560], P(('dp', 'mp'))
- labels: bfloat16 [16384, 1024], P(('dp', 'mp')), may hold values from -12 to 12
- candidates: int32 [256, 8], P(('dp', 'mp')), may hold values from 0 to 127, as said below
- counts: int32 [256], P(('dp', 'mp')), may hold values from 4 to 8, as said below
- home: int32 [128], replicated, may hold values from 0 to 127, as said below
Outputs:
- profiles: bfloat16 [65536, 1024], P(('dp', 'mp'))
The draws below stay inside these ranges and needn't reach their ends.
Inputs may be any that keep to these rules, and one draw needn't show every extreme that they name: `home`: a permutation of the tiles. `candidates`: candidate tile ids are distinct within a block; entries from position counts[b] on are padding; the candidate tiles of the 8 blocks of one device, padding included, are exactly one tile stored on each device with the same mp index. `counts`: some block of every device has 8.
All inputs are finite; a program needn't handle non-finite values.
Results may differ from the reference program's by a relative error of at most 0.0048.
Values may be sent and summed in bfloat16 or wider, within the bound.
A program may use at most 192 MiB of HBM per device.

```python
import math
import jax
import jax.numpy as jnp
from jax import lax

D = 2560
LAB = 1024
TR = 128
BR = 256
CAND = 8
CMIN = 4
TILE_DEV = 4
BLK_DEV = 8
TILES = 128
BLOCKS = 256
TOKENS = 65536
N_DP = 8
N_MP = 4
DEVICES = 32


def routing(key):
    base = jax.random.fold_in(key, 101)
    home = jax.random.permutation(jax.random.fold_in(base, 1), TILES).astype(jnp.int32)
    inverse = jnp.zeros((TILES,), jnp.int32).at[home].set(jnp.arange(TILES, dtype=jnp.int32))
    picks = jax.random.randint(jax.random.fold_in(base, 2), (DEVICES, N_DP), 0, TILE_DEV).astype(jnp.int32)
    pool_keys = jax.random.split(jax.random.fold_in(base, 3), DEVICES)
    pools = jax.vmap(lambda k: jax.random.permutation(k, N_DP))(pool_keys).astype(jnp.int32)
    rest_keys = jax.random.split(jax.random.fold_in(base, 4), BLOCKS)
    rests = jax.vmap(lambda k: jax.random.permutation(k, N_DP - CMIN)[:CAND - CMIN])(rest_keys).astype(jnp.int32)
    block_ids = jnp.arange(BLOCKS, dtype=jnp.int32)
    device = block_ids // BLK_DEV
    within = block_ids % BLK_DEV
    first = within[:, None] * CMIN + jnp.arange(CMIN, dtype=jnp.int32)[None, :]
    later = within[:, None] * CMIN + CMIN + rests
    position = jnp.concatenate([first, later], axis=1) % N_DP
    owner = jnp.take_along_axis(pools[device], position, axis=1)
    column = device % N_MP
    local = jnp.take_along_axis(picks[device], owner, axis=1)
    storage = (owner * N_MP + column[:, None]) * TILE_DEV + local
    candidates = inverse[storage]
    live_counts = jax.random.randint(jax.random.fold_in(base, 5), (BLOCKS,), CMIN, CAND + 1).astype(jnp.int32)
    fullest = jax.random.randint(jax.random.fold_in(base, 6), (DEVICES,), 0, BLK_DEV).astype(jnp.int32)
    live_counts = jnp.where(within == fullest[device], CAND, live_counts).astype(jnp.int32)
    return (home, candidates.astype(jnp.int32), live_counts)


def centroid_parts(key):
    base = jax.random.fold_in(key, 202)
    raw = jax.random.normal(jax.random.fold_in(base, 1), (TILES * TR, D), jnp.float32)
    logscale = jax.random.uniform(jax.random.fold_in(base, 2), (TILES * TR, 1), jnp.float32, math.log(0.5), math.log(1.5))
    scales = jnp.exp(logscale)
    return raw * scales


def draw_home(key, part):
    return routing(key)[0]


def draw_candidates(key, part):
    return routing(key)[1]


def draw_counts(key, part):
    return routing(key)[2]


def draw_centroids(key, part):
    return centroid_parts(key).astype(jnp.bfloat16)


def draw_embeddings(key, part):
    base = jax.random.fold_in(key, 303)
    values = jax.random.normal(jax.random.fold_in(base, 1), (TOKENS, D), jnp.float32)
    return values.astype(jnp.bfloat16)


def levels(own_key, extent, shards, low, top_value):
    gain, own = 1.0, jax.random.fold_in(own_key, 6)
    for dim, blocks in shards:
        steps = jnp.exp(jax.random.uniform(jax.random.fold_in(own, dim), (blocks,), jnp.float32, low / len(shards), top_value / len(shards)))
        gain = gain * jnp.repeat(steps, extent[dim] // blocks).reshape([-1 if axis == dim else 1 for axis in range(len(extent))])
    return gain


def noise(own_key, extent, scale, most, pieces=(), kind=jnp.bfloat16):
    factor_of = levels(own_key, extent, pieces, -0.22, 0.18) if pieces else 1.0
    drawn = jax.random.normal(own_key, extent, jnp.float32) * scale * factor_of
    return jnp.minimum(jnp.maximum(drawn, -most), most).astype(kind)


def setup_inputs(seed: int = 0) -> dict:
    splits = jax.random.split(jax.random.key(seed), 7)
    return {
        "embeddings": draw_embeddings(jax.random.fold_in(splits[6], 71), 0),
        "centroids": draw_centroids(jax.random.fold_in(splits[6], 71), 0),
        "labels": noise(splits[2], (TILES * TR, LAB), 2.0, 12.0, ((0, 32),)),
        "candidates": draw_candidates(jax.random.fold_in(splits[6], 71), 0),
        "counts": draw_counts(jax.random.fold_in(splits[6], 71), 0),
        "home": draw_home(jax.random.fold_in(splits[6], 71), 0),
    }


def reference(embeddings, centroids, labels, candidates, counts, home):
    tile_total = home.shape[0]
    cent_tiles = centroids.reshape(tile_total, TR, D)
    label_tiles = labels.reshape(tile_total, TR, LAB)
    storage = home[candidates].astype(jnp.int32)
    block_rows = embeddings.reshape(BLOCKS, BR, D)
    scale = 2.0 / math.sqrt(D)

    def one_block(items):
        rows, slots, count = items
        chosen = cent_tiles[slots].astype(jnp.float32)
        chosen_labels = label_tiles[slots].astype(jnp.float32)
        logits = jnp.einsum('rd,ctd->rct', rows.astype(jnp.float32), chosen) * scale
        live = (jnp.arange(CAND, dtype=jnp.int32) < count)[None, :, None]
        logits = jnp.where(live, logits, -jnp.inf)
        peak = lax.optimization_barrier(jnp.max(logits, axis=(1, 2), keepdims=True))
        weights = jnp.exp(logits - peak)
        total = lax.optimization_barrier(jnp.sum(weights, axis=(1, 2), keepdims=True))
        probs = (weights / total).astype(jnp.bfloat16)
        result = jnp.einsum('rct,ctl->rl', probs.astype(jnp.float32), chosen_labels)
        return result.astype(jnp.bfloat16)
    result = lax.map(one_block, (block_rows, storage, counts))
    return result.reshape(BLOCKS * BR, LAB)
```

```python
import functools
import math

import jax
import jax.numpy as jnp
from jax import lax
from jax.experimental import pallas as pl
from jax.experimental.pallas import tpu as pltpu
from jax.sharding import PartitionSpec as P

TR = 128
BR = 256
UNIT = 256
TAIL = (128, 64, 64)
EARLY = 2
MESH = pl.DeviceIdType.MESH
VMEM_BYTES = 62 * 1024 * 1024
CLOSE_BYTES = 14 * 1024 * 1024


def products(members, features):
    return lax.dot_general(
        members, features, (((1,), (1,)), ((), ())), preferred_element_type=jnp.float32
    )


def profile_of(raw, pool_ref, width, live, scale, logits):
    here = pl.ds(0, raw.shape[0])
    logits[here, :] = jnp.where(live > 0, raw * scale, -jnp.inf)
    values = logits[here, :]
    peak = jnp.max(values, axis=1, keepdims=True)
    weights = jnp.exp(values - peak)
    total = jnp.sum(weights, axis=1, keepdims=True)
    probs = (weights / total).astype(jnp.bfloat16)
    label_columns = pl.ds(width, pool_ref.shape[1] - width)
    profile = jnp.dot(probs, pool_ref[:, label_columns], preferred_element_type=jnp.float32)
    return profile.astype(jnp.bfloat16)


def pieces_of(row_count):
    whole = row_count - sum(TAIL)
    sizes = [UNIT] * (whole // UNIT) + list(TAIL)
    starts = [sum(sizes[:i]) for i in range(len(sizes))]
    return list(zip(starts, sizes))


def close_kernel(count_mp, scale, held_ref, rows_ref, pool_ref, live_ref, rest_ref, out_ref, logits, result, sem):
    pieces = pieces_of(out_ref.shape[0])
    copies = [
        pltpu.make_async_copy(held_ref.at[pl.ds(*piece), :], out_ref.at[pl.ds(*piece), :], sem.at[i])
        for i, piece in enumerate(pieces[:-1])
    ]
    for copy in copies:
        copy.start()
    last = pl.ds(*pieces[-1])
    width = rows_ref.shape[1]
    part = width // count_mp
    half = count_mp // 2
    side = lax.axis_index("mp") // half
    late = pl.ds(pl.multiple_of((half - side) * part, part), part)
    raw = rest_ref[...] + products(rows_ref[last, late], pool_ref[:, late])
    result[...] = profile_of(raw, pool_ref, width, live_ref[pl.ds(0, 1), :], scale, logits)
    final = pltpu.make_async_copy(result, out_ref.at[last, :], sem.at[len(copies)])
    final.start()
    for copy in copies + [final]:
        copy.wait()


def kernel(
    count_dp,
    count_mp,
    scale,
    cand_hbm,
    count_hbm,
    home_hbm,
    emb_ref,
    cent_ref,
    label_ref,
    out_ref,
    rows,
    pool,
    last_live,
    last_rest,
    cand_ref,
    count_ref,
    home_ref,
    stored,
    staging,
    ids_out,
    ids_in,
    logits,
    row_send,
    row_recv,
    id_send,
    id_recv,
    ready,
    tile_send,
    tile_recv,
    local_sem,
):
    my_dp = lax.axis_index("dp")
    my_mp = lax.axis_index("mp")
    blocks, cands = cand_ref.shape
    pieces = pieces_of(blocks * BR)
    units = len(pieces) - len(TAIL)
    part = emb_ref.shape[1]
    tile_count = stored.shape[0]
    width = cent_ref.shape[2]
    label_width = label_ref.shape[2]
    slots = staging.shape[0]
    half = count_mp // 2
    side = my_mp // half
    place = my_mp % half

    edge = half - 1 + side
    opposite = half - side
    at_edge = my_mp == edge
    outers = [side * (half + 1) + i for i in range(half - 1)]
    others = [(1 - side) * (half + 1) + i for i in range(half - 1)]
    barrier = pltpu.get_barrier_semaphore()

    def tell(dp, mp):
        pl.semaphore_signal(barrier, inc=1, device_id=(dp, mp), device_id_type=MESH)

    @pl.when(at_edge)
    def _():
        tell(my_dp, opposite)
        for mp in outers + others:
            tell(my_dp, mp)

        def greet(i, carry):
            for mp in outers:
                tell((my_dp + i) % count_dp, mp)
            return carry

        lax.fori_loop(1, count_dp, greet, 0)

    @pl.when(jnp.logical_not(at_edge))
    def _():
        for mp in others:
            tell(my_dp, mp)
        for i in range(1, half - 1):
            tell(my_dp, side * (half + 1) + (my_mp - side * (half + 1) + i) % (half - 1))

        def greet(i, carry):
            tell((my_dp + i) % count_dp, my_mp)
            return carry

        lax.fori_loop(1, count_dp, greet, 0)

    own_columns = pl.ds(pl.multiple_of(my_mp * part, part), part)
    here = [
        pltpu.make_async_copy(cent_ref, stored.at[:, :, pl.ds(0, width)], local_sem.at[0]),
        pltpu.make_async_copy(label_ref, stored.at[:, :, pl.ds(width, label_width)], local_sem.at[1]),
        pltpu.make_async_copy(
            emb_ref.at[pl.ds(pl.multiple_of(my_mp * blocks * BR, BR), blocks * BR), :],
            rows.at[:, own_columns],
            local_sem.at[2],
        ),
        pltpu.make_async_copy(cand_hbm, cand_ref, local_sem.at[3]),
        pltpu.make_async_copy(count_hbm, count_ref, local_sem.at[4]),
        pltpu.make_async_copy(home_hbm, home_ref, local_sem.at[5]),
    ]
    for copy in here:
        copy.start()

    pl.semaphore_wait(barrier, jnp.where(at_edge, 1, count_mp - 1 + 2 * (count_dp - 1)))

    def send_rows(piece, b, target):
        start, size = piece
        return pltpu.make_async_remote_copy(
            src_ref=emb_ref.at[pl.ds(pl.multiple_of(target * blocks * BR + start, size), size), :],
            dst_ref=rows.at[pl.ds(pl.multiple_of(start, size), size), own_columns],
            send_sem=row_send.at[target, b],
            recv_sem=row_recv.at[my_mp, b],
            device_id=(my_dp, target),
            device_id_type=MESH,
        )

    near = [side * half + (place + i) % half for i in range(1, half)]
    far = [(1 - side) * half + (place + i) % half for i in range(half)]
    tail = list(enumerate(pieces))[units:]

    def send_near(b, carry):
        for target in near:
            send_rows((b * UNIT, UNIT), b, target).start()
        return carry

    def send_far(b, carry):
        for target in far:
            send_rows((b * UNIT, UNIT), b, target).start()
        return carry

    @pl.when(at_edge)
    def _():
        for b in range(EARLY):
            send_rows(pieces[b], b, opposite).start()
        pl.semaphore_wait(ready, 1)

    @pl.when(my_mp == edge - 1 + 2 * side)
    def _():
        pl.semaphore_signal(ready, inc=1, device_id=(my_dp, edge), device_id_type=MESH)

    def send_id(i):
        peer = (my_dp + i) % count_dp
        return pltpu.make_async_remote_copy(
            src_ref=ids_out.at[peer],
            dst_ref=ids_in.at[my_dp],
            send_sem=id_send.at[i],
            recv_sem=id_recv.at[i],
            device_id=(peer, my_mp),
            device_id_type=MESH,
        )

    def start_id(i, carry):
        send_id(i).start()
        return carry

    lax.fori_loop(0, units, send_near, 0)
    for b, piece in tail:
        for target in near:
            send_rows(piece, b, target).start()
    for b in range(EARLY):
        for target in far:

            @pl.when(jnp.logical_or(jnp.logical_not(at_edge), target != opposite))
            def _():
                send_rows(pieces[b], b, target).start()

    lax.fori_loop(EARLY, units, send_far, 0)
    for target in far:
        for b, piece in tail:
            send_rows(piece, b, target).start()
    for copy in here[3:]:
        copy.wait()
    peer_ids = lax.broadcasted_iota(jnp.int32, ids_out.shape, 0)

    def want(b, carry):
        for j in range(cands):
            cell = home_ref[cand_ref[b, j]]
            carry = jnp.where(peer_ids == cell // (tile_count * count_mp), cell % tile_count, carry)
        return carry

    ids_out[...] = lax.fori_loop(0, blocks, want, jnp.zeros(ids_out.shape, jnp.int32))

    for copy in here[:2]:
        copy.wait()
    lax.fori_loop(1, count_dp, start_id, 0)

    my_tile = pl.ds(pl.multiple_of(my_dp * TR, TR), TR)

    def send_tile(i):
        return pltpu.make_async_remote_copy(
            src_ref=staging.at[(i - 1) % slots],
            dst_ref=pool.at[my_tile, :],
            send_sem=tile_send.at[i],
            recv_sem=tile_recv.at[i],
            device_id=((my_dp + count_dp - i) % count_dp, my_mp),
            device_id_type=MESH,
        )

    def stage(i, carry):
        send_id(i).wait_recv()
        index = jnp.max(ids_in[(my_dp + count_dp - i) % count_dp])

        @pl.when(i > slots)
        def _():
            send_tile(i - slots).wait_send()

        staging[(i - 1) % slots] = stored[index]

        @pl.when(i > 1)
        def _():
            send_tile(i - 1).start()

        return carry

    lax.fori_loop(1, count_dp, stage, 0)
    pool[my_tile, :] = stored[jnp.max(ids_out[my_dp])]
    send_tile(count_dp - 1).start()

    def tile_arrives(i, carry):
        send_tile(i).wait_recv()
        return carry

    lax.fori_loop(1, count_dp, tile_arrives, 0)
    here[2].wait()

    def rows_arrive(piece, b, sources):
        start, size = piece
        for source in sources:
            pltpu.make_async_remote_copy(
                src_ref=emb_ref.at[pl.ds(0, size), :],
                dst_ref=rows.at[
                    pl.ds(pl.multiple_of(start, size), size),
                    pl.ds(pl.multiple_of(source * part, part), part),
                ],
                send_sem=row_send.at[source, b],
                recv_sem=row_recv.at[source, b],
                device_id=(my_dp, source),
                device_id_type=MESH,
            ).wait_recv()

    def live_of(block, shape):
        count = count_ref[block]
        column_peer = lax.broadcasted_iota(jnp.int32, shape, 1) // TR
        live = jnp.zeros(shape, jnp.int32)
        for j in range(cands):
            slot = home_ref[cand_ref[block, j]] // (tile_count * count_mp)
            slot = jnp.where(j < count, slot, -1)
            live = jnp.where(column_peer == slot, 1, live)
        return live

    last_live[...] = live_of(blocks - 1, last_live.shape)

    def score(piece, live):
        mine = pl.ds(pl.multiple_of(piece[0], piece[1]), piece[1])
        raw = products(rows[mine, :], pool[:, pl.ds(0, width)])
        out_ref[mine, :] = profile_of(raw, pool, width, live, scale, logits)

    def score_unit(b, carry):
        piece = (b * UNIT, UNIT)
        rows_arrive(piece, b, near + far)
        score(piece, live_of(b, (1, count_dp * TR)))
        return carry

    lax.fori_loop(0, units, score_unit, 0)
    b, piece = tail[-1]
    early_far = [(1 - side) * (half + 1) + i for i in range(half - 1)]
    rows_arrive(piece, b, near + early_far)
    last = pl.ds(*piece)
    same = pl.ds(pl.multiple_of(side * half * part, part), half * part)
    beyond = pl.ds(pl.multiple_of((1 - side) * (half + 1) * part, part), (half - 1) * part)
    last_rest[...] = products(rows[last, same], pool[:, same]) + products(rows[last, beyond], pool[:, beyond])
    for b, piece in tail[:-1]:
        rows_arrive(piece, b, near + far)
        score(piece, last_live[pl.ds(0, 1), :])
    b, piece = tail[-1]
    rows_arrive(piece, b, [opposite])

    def finish_rows(b, carry):
        for target in near + far:
            send_rows((b * UNIT, UNIT), b, target).wait_send()
        return carry

    lax.fori_loop(0, units, finish_rows, 0)
    for b, piece in tail:
        for target in near + far:
            send_rows(piece, b, target).wait_send()

    def finish_ids(i, carry):
        send_id(i).wait_send()
        return carry

    lax.fori_loop(1, count_dp, finish_ids, 0)

    def finish_tiles(i, carry):
        send_tile(i).wait_send()
        return carry

    lax.fori_loop(max(count_dp - slots, 1), count_dp, finish_tiles, 0)


def body(embeddings, centroids, labels, candidates, counts, home):
    count_dp = lax.axis_size("dp")
    count_mp = lax.axis_size("mp")
    part = embeddings.shape[1]
    width = centroids.shape[1]
    label_width = labels.shape[1]
    tile_count = centroids.shape[0] // TR
    blocks, cands = candidates.shape
    row_count = blocks * BR
    pieces = pieces_of(row_count)
    last_size = pieces[-1][1]
    both = width + label_width
    slots = count_dp - 1 if count_dp <= 8 else 3
    anywhere = pl.BlockSpec(memory_space=pl.ANY)
    local = pl.BlockSpec(memory_space=pltpu.VMEM)
    scale = 2.0 / math.sqrt(width)
    handed = [
        pltpu.VMEM((row_count - last_size, label_width), jnp.bfloat16),
        pltpu.VMEM((row_count, width), jnp.bfloat16),
        pltpu.VMEM((count_dp * TR, both), jnp.bfloat16),
        pltpu.VMEM((8, count_dp * TR), jnp.int32),
        pltpu.VMEM((last_size, count_dp * TR), jnp.float32),
    ]
    handed_bytes = 2 * ((row_count - last_size) * label_width + row_count * width) + count_dp * TR * (2 * both + 32 + 4 * last_size)
    held = pl.pallas_call(
        functools.partial(kernel, count_dp, count_mp, scale),
        in_specs=[anywhere] * 6,
        out_specs=[local] * len(handed),
        out_shape=handed,
        scratch_shapes=[
            pltpu.SMEM(candidates.shape, jnp.int32),
            pltpu.SMEM(counts.shape, jnp.int32),
            pltpu.SMEM(home.shape, jnp.int32),
            pltpu.VMEM((tile_count, TR, both), jnp.bfloat16),
            pltpu.VMEM((slots, TR, both), jnp.bfloat16),
            pltpu.VMEM((count_dp, 8, 128), jnp.int32),
            pltpu.VMEM((count_dp, 8, 128), jnp.int32),
            pltpu.VMEM((UNIT, count_dp * TR), jnp.float32),
            pltpu.SemaphoreType.DMA((count_mp, len(pieces))),
            pltpu.SemaphoreType.DMA((count_mp, len(pieces))),
            pltpu.SemaphoreType.DMA((count_dp,)),
            pltpu.SemaphoreType.DMA((count_dp,)),
            pltpu.SemaphoreType.REGULAR,
            pltpu.SemaphoreType.DMA((count_dp,)),
            pltpu.SemaphoreType.DMA((count_dp,)),
            pltpu.SemaphoreType.DMA((6,)),
        ],
        compiler_params=pltpu.CompilerParams(
            collective_id=0, has_side_effects=True, vmem_limit_bytes=VMEM_BYTES - handed_bytes
        ),
        name="annotate",
    )(
        candidates,
        counts,
        home,
        embeddings,
        centroids.reshape(tile_count, TR, width),
        labels.reshape(tile_count, TR, label_width),
    )
    return pl.pallas_call(
        functools.partial(close_kernel, count_mp, scale),
        in_specs=[local] * len(handed),
        out_specs=anywhere,
        out_shape=jax.ShapeDtypeStruct((row_count, label_width), jnp.bfloat16),
        scratch_shapes=[
            pltpu.VMEM((last_size, count_dp * TR), jnp.float32),
            pltpu.VMEM((last_size, label_width), jnp.bfloat16),
            pltpu.SemaphoreType.DMA((len(pieces),)),
        ],
        compiler_params=pltpu.CompilerParams(vmem_limit_bytes=CLOSE_BYTES),
        name="close",
    )(*[pltpu.with_memory_space_constraint(value, pltpu.VMEM) for value in held])


def solution(mesh):
    placed = (
        P("dp", "mp"),
        P(("dp", "mp"), None),
        P(("dp", "mp"), None),
        P(("dp", "mp"), None),
        P(("dp", "mp")),
        P(),
    )
    return jax.shard_map(
        body, mesh=mesh, in_specs=placed, out_specs=P(("dp", "mp"), None), check_vma=False
    )
```

```python
import functools
import math

import jax
import jax.numpy as jnp
from jax import lax
from jax.experimental import pallas as pl
from jax.experimental.pallas import tpu as pltpu
from jax.sharding import PartitionSpec as P

TR = 128
BR = 256
UNIT = 256
TAIL = (128, 128)
ALIGN = 64
EARLY = 2
MESH = pl.DeviceIdType.MESH
VMEM_BYTES = 62 * 1024 * 1024
CLOSE_BYTES = 14 * 1024 * 1024


def products(members, features):
    return lax.dot_general(
        members, features, (((1,), (1,)), ((), ())), preferred_element_type=jnp.float32
    )


def profile_of(raw, pool_ref, width, live, scale, logits):
    here = pl.ds(0, raw.shape[0])
    logits[here, :] = jnp.where(live > 0, raw * scale, -jnp.inf)
    values = logits[here, :]
    peak = jnp.max(values, axis=1, keepdims=True)
    weights = jnp.exp(values - peak)
    total = jnp.sum(weights, axis=1, keepdims=True)
    probs = (weights / total).astype(jnp.bfloat16)
    label_columns = pl.ds(width, pool_ref.shape[1] - width)
    profile = jnp.dot(probs, pool_ref[:, label_columns], preferred_element_type=jnp.float32)
    return profile.astype(jnp.bfloat16)


def pieces_of(row_count):
    whole = row_count - sum(TAIL)
    sizes = [UNIT] * (whole // UNIT) + list(TAIL)
    starts = [sum(sizes[:i]) for i in range(len(sizes))]
    return list(zip(starts, sizes))


def close_kernel(count_mp, scale, held_ref, rows_ref, pool_ref, live_ref, rest_ref, out_ref, logits, result, sem):
    pieces = pieces_of(out_ref.shape[0])
    copies = [
        pltpu.make_async_copy(held_ref.at[pl.ds(*piece), :], out_ref.at[pl.ds(*piece), :], sem.at[i])
        for i, piece in enumerate(pieces[:-1])
    ]
    for copy in copies:
        copy.start()
    last = pl.ds(*pieces[-1])
    width = rows_ref.shape[1]
    part = width // count_mp
    half = count_mp // 2
    side = lax.axis_index("mp") // half
    late = pl.ds(pl.multiple_of((half - side) * part, part), part)
    raw = rest_ref[...] + products(rows_ref[last, late], pool_ref[:, late])
    result[...] = profile_of(raw, pool_ref, width, live_ref[pl.ds(0, 1), :], scale, logits)
    final = pltpu.make_async_copy(result, out_ref.at[last, :], sem.at[len(copies)])
    final.start()
    for copy in copies + [final]:
        copy.wait()


def kernel(
    count_dp,
    count_mp,
    scale,
    cand_hbm,
    count_hbm,
    home_hbm,
    emb_ref,
    cent_ref,
    label_ref,
    out_ref,
    rows,
    pool,
    last_live,
    last_rest,
    cand_ref,
    count_ref,
    home_ref,
    stored,
    staging,
    ids_out,
    ids_in,
    logits,
    row_send,
    row_recv,
    id_send,
    id_recv,
    ready,
    tile_send,
    tile_recv,
    local_sem,
):
    my_dp = lax.axis_index("dp")
    my_mp = lax.axis_index("mp")
    blocks, cands = cand_ref.shape
    pieces = pieces_of(blocks * BR)
    units = len(pieces) - len(TAIL)
    part = emb_ref.shape[1]
    tile_count = stored.shape[0]
    width = cent_ref.shape[2]
    label_width = label_ref.shape[2]
    slots = staging.shape[0]
    half = count_mp // 2
    side = my_mp // half
    place = my_mp % half

    edge = half - 1 + side
    opposite = half - side
    at_edge = my_mp == edge
    outers = [side * (half + 1) + i for i in range(half - 1)]
    others = [(1 - side) * (half + 1) + i for i in range(half - 1)]
    barrier = pltpu.get_barrier_semaphore()

    def tell(dp, mp):
        pl.semaphore_signal(barrier, inc=1, device_id=(dp, mp), device_id_type=MESH)

    @pl.when(at_edge)
    def _():
        tell(my_dp, opposite)
        for mp in outers + others:
            tell(my_dp, mp)

        def greet(i, carry):
            for mp in outers:
                tell((my_dp + i) % count_dp, mp)
            return carry

        lax.fori_loop(1, count_dp, greet, 0)

    @pl.when(jnp.logical_not(at_edge))
    def _():
        for mp in others:
            tell(my_dp, mp)
        for i in range(1, half - 1):
            tell(my_dp, side * (half + 1) + (my_mp - side * (half + 1) + i) % (half - 1))

        def greet(i, carry):
            tell((my_dp + i) % count_dp, my_mp)
            return carry

        lax.fori_loop(1, count_dp, greet, 0)

    own_columns = pl.ds(pl.multiple_of(my_mp * part, part), part)
    here = [
        pltpu.make_async_copy(cent_ref, stored.at[:, :, pl.ds(0, width)], local_sem.at[0]),
        pltpu.make_async_copy(label_ref, stored.at[:, :, pl.ds(width, label_width)], local_sem.at[1]),
        pltpu.make_async_copy(
            emb_ref.at[pl.ds(pl.multiple_of(my_mp * blocks * BR, BR), blocks * BR), :],
            rows.at[:, own_columns],
            local_sem.at[2],
        ),
        pltpu.make_async_copy(cand_hbm, cand_ref, local_sem.at[3]),
        pltpu.make_async_copy(count_hbm, count_ref, local_sem.at[4]),
        pltpu.make_async_copy(home_hbm, home_ref, local_sem.at[5]),
    ]
    for copy in here:
        copy.start()

    pl.semaphore_wait(barrier, jnp.where(at_edge, 1, count_mp - 1 + 2 * (count_dp - 1)))

    def send_rows(piece, b, target):
        start, size = piece
        return pltpu.make_async_remote_copy(
            src_ref=emb_ref.at[pl.ds(pl.multiple_of(target * blocks * BR + start, ALIGN), size), :],
            dst_ref=rows.at[pl.ds(pl.multiple_of(start, ALIGN), size), own_columns],
            send_sem=row_send.at[target, b],
            recv_sem=row_recv.at[my_mp, b],
            device_id=(my_dp, target),
            device_id_type=MESH,
        )

    near = [side * half + (place + i) % half for i in range(1, half)]
    far = [(1 - side) * half + (place + i) % half for i in range(half)]
    tail = list(enumerate(pieces))[units:]

    def send_near(b, carry):
        for target in near:
            send_rows((b * UNIT, UNIT), b, target).start()
        return carry

    def send_far(b, carry):
        for target in far:
            send_rows((b * UNIT, UNIT), b, target).start()
        return carry

    @pl.when(at_edge)
    def _():
        for b in range(EARLY):
            send_rows(pieces[b], b, opposite).start()
        pl.semaphore_wait(ready, 1)

    @pl.when(my_mp == edge - 1 + 2 * side)
    def _():
        pl.semaphore_signal(ready, inc=1, device_id=(my_dp, edge), device_id_type=MESH)

    def send_id(i):
        peer = (my_dp + i) % count_dp
        return pltpu.make_async_remote_copy(
            src_ref=ids_out.at[peer],
            dst_ref=ids_in.at[my_dp],
            send_sem=id_send.at[i],
            recv_sem=id_recv.at[i],
            device_id=(peer, my_mp),
            device_id_type=MESH,
        )

    def start_id(i, carry):
        send_id(i).start()
        return carry

    lax.fori_loop(0, units, send_near, 0)
    for b, piece in tail:
        for target in near:
            send_rows(piece, b, target).start()
    for b in range(EARLY):
        for target in far:

            @pl.when(jnp.logical_or(jnp.logical_not(at_edge), target != opposite))
            def _():
                send_rows(pieces[b], b, target).start()

    lax.fori_loop(EARLY, units, send_far, 0)
    for target in far:
        for b, piece in tail:
            send_rows(piece, b, target).start()
    for copy in here[3:]:
        copy.wait()
    peer_ids = lax.broadcasted_iota(jnp.int32, ids_out.shape, 0)

    def want(b, carry):
        for j in range(cands):
            cell = home_ref[cand_ref[b, j]]
            carry = jnp.where(peer_ids == cell // (tile_count * count_mp), cell % tile_count, carry)
        return carry

    ids_out[...] = lax.fori_loop(0, blocks, want, jnp.zeros(ids_out.shape, jnp.int32))

    for copy in here[:2]:
        copy.wait()
    lax.fori_loop(1, count_dp, start_id, 0)

    my_tile = pl.ds(pl.multiple_of(my_dp * TR, TR), TR)

    def send_tile(i):
        return pltpu.make_async_remote_copy(
            src_ref=staging.at[(i - 1) % slots],
            dst_ref=pool.at[my_tile, :],
            send_sem=tile_send.at[i],
            recv_sem=tile_recv.at[i],
            device_id=((my_dp + count_dp - i) % count_dp, my_mp),
            device_id_type=MESH,
        )

    def stage(i, carry):
        send_id(i).wait_recv()
        index = jnp.max(ids_in[(my_dp + count_dp - i) % count_dp])

        @pl.when(i > slots)
        def _():
            send_tile(i - slots).wait_send()

        staging[(i - 1) % slots] = stored[index]

        @pl.when(i > 1)
        def _():
            send_tile(i - 1).start()

        return carry

    lax.fori_loop(1, count_dp, stage, 0)
    pool[my_tile, :] = stored[jnp.max(ids_out[my_dp])]
    send_tile(count_dp - 1).start()

    def tile_arrives(i, carry):
        send_tile(i).wait_recv()
        return carry

    lax.fori_loop(1, count_dp, tile_arrives, 0)
    here[2].wait()

    def rows_arrive(piece, b, sources):
        start, size = piece
        for source in sources:
            pltpu.make_async_remote_copy(
                src_ref=emb_ref.at[pl.ds(0, size), :],
                dst_ref=rows.at[
                    pl.ds(pl.multiple_of(start, ALIGN), size),
                    pl.ds(pl.multiple_of(source * part, part), part),
                ],
                send_sem=row_send.at[source, b],
                recv_sem=row_recv.at[source, b],
                device_id=(my_dp, source),
                device_id_type=MESH,
            ).wait_recv()

    def live_of(block, shape):
        count = count_ref[block]
        column_peer = lax.broadcasted_iota(jnp.int32, shape, 1) // TR
        live = jnp.zeros(shape, jnp.int32)
        for j in range(cands):
            slot = home_ref[cand_ref[block, j]] // (tile_count * count_mp)
            slot = jnp.where(j < count, slot, -1)
            live = jnp.where(column_peer == slot, 1, live)
        return live

    last_live[...] = live_of(blocks - 1, last_live.shape)

    def score(piece, live):
        mine = pl.ds(pl.multiple_of(piece[0], ALIGN), piece[1])
        raw = products(rows[mine, :], pool[:, pl.ds(0, width)])
        out_ref[mine, :] = profile_of(raw, pool, width, live, scale, logits)

    def score_unit(b, carry):
        piece = (b * UNIT, UNIT)
        rows_arrive(piece, b, near + far)
        score(piece, live_of(b, (1, count_dp * TR)))
        return carry

    lax.fori_loop(0, units, score_unit, 0)
    b, piece = tail[-1]
    early_far = [(1 - side) * (half + 1) + i for i in range(half - 1)]
    rows_arrive(piece, b, near + early_far)
    last = pl.ds(*piece)
    same = pl.ds(pl.multiple_of(side * half * part, part), half * part)
    beyond = pl.ds(pl.multiple_of((1 - side) * (half + 1) * part, part), (half - 1) * part)
    last_rest[...] = products(rows[last, same], pool[:, same]) + products(rows[last, beyond], pool[:, beyond])
    for b, piece in tail[:-1]:
        rows_arrive(piece, b, near + far)
        score(piece, last_live[pl.ds(0, 1), :])
    b, piece = tail[-1]
    rows_arrive(piece, b, [opposite])

    def finish_rows(b, carry):
        for target in near + far:
            send_rows((b * UNIT, UNIT), b, target).wait_send()
        return carry

    lax.fori_loop(0, units, finish_rows, 0)
    for b, piece in tail:
        for target in near + far:
            send_rows(piece, b, target).wait_send()

    def finish_ids(i, carry):
        send_id(i).wait_send()
        return carry

    lax.fori_loop(1, count_dp, finish_ids, 0)

    def finish_tiles(i, carry):
        send_tile(i).wait_send()
        return carry

    lax.fori_loop(max(count_dp - slots, 1), count_dp, finish_tiles, 0)


def body(embeddings, centroids, labels, candidates, counts, home):
    count_dp = lax.axis_size("dp")
    count_mp = lax.axis_size("mp")
    part = embeddings.shape[1]
    width = centroids.shape[1]
    label_width = labels.shape[1]
    tile_count = centroids.shape[0] // TR
    blocks, cands = candidates.shape
    row_count = blocks * BR
    pieces = pieces_of(row_count)
    last_size = pieces[-1][1]
    both = width + label_width
    slots = count_dp - 1 if count_dp <= 8 else 3
    anywhere = pl.BlockSpec(memory_space=pl.ANY)
    local = pl.BlockSpec(memory_space=pltpu.VMEM)
    scale = 2.0 / math.sqrt(width)
    handed = [
        pltpu.VMEM((row_count - last_size, label_width), jnp.bfloat16),
        pltpu.VMEM((row_count, width), jnp.bfloat16),
        pltpu.VMEM((count_dp * TR, both), jnp.bfloat16),
        pltpu.VMEM((8, count_dp * TR), jnp.int32),
        pltpu.VMEM((last_size, count_dp * TR), jnp.float32),
    ]
    handed_bytes = 2 * ((row_count - last_size) * label_width + row_count * width) + count_dp * TR * (2 * both + 32 + 4 * last_size)
    held = pl.pallas_call(
        functools.partial(kernel, count_dp, count_mp, scale),
        in_specs=[anywhere] * 6,
        out_specs=[local] * len(handed),
        out_shape=handed,
        scratch_shapes=[
            pltpu.SMEM(candidates.shape, jnp.int32),
            pltpu.SMEM(counts.shape, jnp.int32),
            pltpu.SMEM(home.shape, jnp.int32),
            pltpu.VMEM((tile_count, TR, both), jnp.bfloat16),
            pltpu.VMEM((slots, TR, both), jnp.bfloat16),
            pltpu.VMEM((count_dp, 8, 128), jnp.int32),
            pltpu.VMEM((count_dp, 8, 128), jnp.int32),
            pltpu.VMEM((UNIT, count_dp * TR), jnp.float32),
            pltpu.SemaphoreType.DMA((count_mp, len(pieces))),
            pltpu.SemaphoreType.DMA((count_mp, len(pieces))),
            pltpu.SemaphoreType.DMA((count_dp,)),
            pltpu.SemaphoreType.DMA((count_dp,)),
            pltpu.SemaphoreType.REGULAR,
            pltpu.SemaphoreType.DMA((count_dp,)),
            pltpu.SemaphoreType.DMA((count_dp,)),
            pltpu.SemaphoreType.DMA((6,)),
        ],
        compiler_params=pltpu.CompilerParams(
            collective_id=0, has_side_effects=True, vmem_limit_bytes=VMEM_BYTES - handed_bytes
        ),
        name="annotate",
    )(
        candidates,
        counts,
        home,
        embeddings,
        centroids.reshape(tile_count, TR, width),
        labels.reshape(tile_count, TR, label_width),
    )
    return pl.pallas_call(
        functools.partial(close_kernel, count_mp, scale),
        in_specs=[local] * len(handed),
        out_specs=anywhere,
        out_shape=jax.ShapeDtypeStruct((row_count, label_width), jnp.bfloat16),
        scratch_shapes=[
            pltpu.VMEM((last_size, count_dp * TR), jnp.float32),
            pltpu.VMEM((last_size, label_width), jnp.bfloat16),
            pltpu.SemaphoreType.DMA((len(pieces),)),
        ],
        compiler_params=pltpu.CompilerParams(vmem_limit_bytes=CLOSE_BYTES),
        name="close",
    )(*[pltpu.with_memory_space_constraint(value, pltpu.VMEM) for value in held])


def solution(mesh):
    placed = (
        P("dp", "mp"),
        P(("dp", "mp"), None),
        P(("dp", "mp"), None),
        P(("dp", "mp"), None),
        P(("dp", "mp")),
        P(),
    )
    return jax.shard_map(
        body, mesh=mesh, in_specs=placed, out_specs=P(("dp", "mp"), None), check_vma=False
    )
```

```python
import functools
import math

import jax
import jax.numpy as jnp
from jax import lax
from jax.experimental import pallas as pl
from jax.experimental.pallas import tpu as pltpu
from jax.sharding import PartitionSpec as P

TR = 128
BR = 256
UNIT = 256
TAIL = (128, 128)
ALIGN = 64
MESH = pl.DeviceIdType.MESH
VMEM_BYTES = 62 * 1024 * 1024
CLOSE_BYTES = 14 * 1024 * 1024


def products(members, features):
    return lax.dot_general(
        members, features, (((1,), (1,)), ((), ())), preferred_element_type=jnp.float32
    )


def profile_of(raw, pool_ref, width, live, scale, logits):
    here = pl.ds(0, raw.shape[0])
    logits[here, :] = jnp.where(live > 0, raw * scale, -jnp.inf)
    values = logits[here, :]
    peak = jnp.max(values, axis=1, keepdims=True)
    weights = jnp.exp(values - peak)
    total = jnp.sum(weights, axis=1, keepdims=True)
    probs = (weights / total).astype(jnp.bfloat16)
    label_columns = pl.ds(width, pool_ref.shape[1] - width)
    profile = jnp.dot(probs, pool_ref[:, label_columns], preferred_element_type=jnp.float32)
    return profile.astype(jnp.bfloat16)


def pieces_of(row_count):
    left = row_count // UNIT
    sizes = []
    while left > 1:
        sizes.append(left // 2 * UNIT)
        left -= left // 2
    sizes += TAIL
    starts = [sum(sizes[:i]) for i in range(len(sizes))]
    return list(zip(starts, sizes))


def close_kernel(count_mp, scale, held_ref, rows_ref, pool_ref, live_ref, rest_ref, out_ref, logits, result, sem):
    pieces = pieces_of(out_ref.shape[0])
    copies = [
        pltpu.make_async_copy(held_ref.at[pl.ds(*piece), :], out_ref.at[pl.ds(*piece), :], sem.at[i])
        for i, piece in enumerate(pieces[:-1])
    ]
    for copy in copies:
        copy.start()
    last = pl.ds(*pieces[-1])
    width = rows_ref.shape[1]
    part = width // count_mp
    half = count_mp // 2
    side = lax.axis_index("mp") // half
    late = pl.ds(pl.multiple_of((half - side) * part, part), part)
    raw = rest_ref[...] + products(rows_ref[last, late], pool_ref[:, late])
    result[...] = profile_of(raw, pool_ref, width, live_ref[pl.ds(0, 1), :], scale, logits)
    final = pltpu.make_async_copy(result, out_ref.at[last, :], sem.at[len(copies)])
    final.start()
    for copy in copies + [final]:
        copy.wait()


def kernel(
    count_dp,
    count_mp,
    scale,
    cand_hbm,
    count_hbm,
    home_hbm,
    emb_ref,
    cent_ref,
    label_ref,
    out_ref,
    rows,
    pool,
    last_live,
    last_rest,
    cand_ref,
    count_ref,
    home_ref,
    stored,
    staging,
    ids_out,
    ids_in,
    logits,
    row_send,
    row_recv,
    id_send,
    id_recv,
    ready,
    tile_send,
    tile_recv,
    local_sem,
):
    my_dp = lax.axis_index("dp")
    my_mp = lax.axis_index("mp")
    blocks, cands = cand_ref.shape
    pieces = pieces_of(blocks * BR)
    bulk = len(pieces) - len(TAIL)
    part = emb_ref.shape[1]
    tile_count = stored.shape[0]
    width = cent_ref.shape[2]
    label_width = label_ref.shape[2]
    slots = staging.shape[0]
    half = count_mp // 2
    side = my_mp // half
    place = my_mp % half

    edge = half - 1 + side
    opposite = half - side
    at_edge = my_mp == edge
    outers = [side * (half + 1) + i for i in range(half - 1)]
    others = [(1 - side) * (half + 1) + i for i in range(half - 1)]
    barrier = pltpu.get_barrier_semaphore()

    def tell(dp, mp):
        pl.semaphore_signal(barrier, inc=1, device_id=(dp, mp), device_id_type=MESH)

    @pl.when(at_edge)
    def _():
        tell(my_dp, opposite)
        for mp in outers + others:
            tell(my_dp, mp)

        def greet(i, carry):
            for mp in outers:
                tell((my_dp + i) % count_dp, mp)
            return carry

        lax.fori_loop(1, count_dp, greet, 0)

    @pl.when(jnp.logical_not(at_edge))
    def _():
        for mp in others:
            tell(my_dp, mp)
        for i in range(1, half - 1):
            tell(my_dp, side * (half + 1) + (my_mp - side * (half + 1) + i) % (half - 1))

        def greet(i, carry):
            tell((my_dp + i) % count_dp, my_mp)
            return carry

        lax.fori_loop(1, count_dp, greet, 0)

    own_columns = pl.ds(pl.multiple_of(my_mp * part, part), part)
    here = [
        pltpu.make_async_copy(cent_ref, stored.at[:, :, pl.ds(0, width)], local_sem.at[0]),
        pltpu.make_async_copy(label_ref, stored.at[:, :, pl.ds(width, label_width)], local_sem.at[1]),
        pltpu.make_async_copy(
            emb_ref.at[pl.ds(pl.multiple_of(my_mp * blocks * BR, BR), blocks * BR), :],
            rows.at[:, own_columns],
            local_sem.at[2],
        ),
        pltpu.make_async_copy(cand_hbm, cand_ref, local_sem.at[3]),
        pltpu.make_async_copy(count_hbm, count_ref, local_sem.at[4]),
        pltpu.make_async_copy(home_hbm, home_ref, local_sem.at[5]),
    ]
    for copy in here:
        copy.start()

    pl.semaphore_wait(barrier, jnp.where(at_edge, 1, count_mp - 1 + 2 * (count_dp - 1)))

    def send_rows(piece, b, target):
        start, size = piece
        return pltpu.make_async_remote_copy(
            src_ref=emb_ref.at[pl.ds(pl.multiple_of(target * blocks * BR + start, ALIGN), size), :],
            dst_ref=rows.at[pl.ds(pl.multiple_of(start, ALIGN), size), own_columns],
            send_sem=row_send.at[target, b],
            recv_sem=row_recv.at[my_mp, b],
            device_id=(my_dp, target),
            device_id_type=MESH,
        )

    near = [side * half + (place + i) % half for i in range(1, half)]
    far = [(1 - side) * half + (place + i) % half for i in range(half)]
    tail = list(enumerate(pieces))[bulk:]

    @pl.when(at_edge)
    def _():
        send_rows(pieces[0], 0, opposite).start()
        pl.semaphore_wait(ready, 1)

    @pl.when(my_mp == edge - 1 + 2 * side)
    def _():
        pl.semaphore_signal(ready, inc=1, device_id=(my_dp, edge), device_id_type=MESH)

    def send_id(i):
        peer = (my_dp + i) % count_dp
        return pltpu.make_async_remote_copy(
            src_ref=ids_out.at[peer],
            dst_ref=ids_in.at[my_dp],
            send_sem=id_send.at[i],
            recv_sem=id_recv.at[i],
            device_id=(peer, my_mp),
            device_id_type=MESH,
        )

    def start_id(i, carry):
        send_id(i).start()
        return carry

    for b, piece in enumerate(pieces):
        for target in near:
            send_rows(piece, b, target).start()
    for target in far:

        @pl.when(jnp.logical_or(jnp.logical_not(at_edge), target != opposite))
        def _():
            send_rows(pieces[0], 0, target).start()

    for b in range(1, bulk):
        for target in far:
            send_rows(pieces[b], b, target).start()
    for target in far:
        for b, piece in tail:
            send_rows(piece, b, target).start()
    for copy in here[3:]:
        copy.wait()
    peer_ids = lax.broadcasted_iota(jnp.int32, ids_out.shape, 0)

    def want(b, carry):
        for j in range(cands):
            cell = home_ref[cand_ref[b, j]]
            carry = jnp.where(peer_ids == cell // (tile_count * count_mp), cell % tile_count, carry)
        return carry

    ids_out[...] = lax.fori_loop(0, blocks, want, jnp.zeros(ids_out.shape, jnp.int32))

    for copy in here[:2]:
        copy.wait()
    lax.fori_loop(1, count_dp, start_id, 0)

    my_tile = pl.ds(pl.multiple_of(my_dp * TR, TR), TR)

    def send_tile(i):
        return pltpu.make_async_remote_copy(
            src_ref=staging.at[(i - 1) % slots],
            dst_ref=pool.at[my_tile, :],
            send_sem=tile_send.at[i],
            recv_sem=tile_recv.at[i],
            device_id=((my_dp + count_dp - i) % count_dp, my_mp),
            device_id_type=MESH,
        )

    def stage(i, carry):
        send_id(i).wait_recv()
        index = jnp.max(ids_in[(my_dp + count_dp - i) % count_dp])

        @pl.when(i > slots)
        def _():
            send_tile(i - slots).wait_send()

        staging[(i - 1) % slots] = stored[index]

        @pl.when(i > 1)
        def _():
            send_tile(i - 1).start()

        return carry

    lax.fori_loop(1, count_dp, stage, 0)
    pool[my_tile, :] = stored[jnp.max(ids_out[my_dp])]
    send_tile(count_dp - 1).start()

    def tile_arrives(i, carry):
        send_tile(i).wait_recv()
        return carry

    lax.fori_loop(1, count_dp, tile_arrives, 0)
    here[2].wait()

    def rows_arrive(piece, b, sources):
        start, size = piece
        for source in sources:
            pltpu.make_async_remote_copy(
                src_ref=emb_ref.at[pl.ds(0, size), :],
                dst_ref=rows.at[
                    pl.ds(pl.multiple_of(start, ALIGN), size),
                    pl.ds(pl.multiple_of(source * part, part), part),
                ],
                send_sem=row_send.at[source, b],
                recv_sem=row_recv.at[source, b],
                device_id=(my_dp, source),
                device_id_type=MESH,
            ).wait_recv()

    def live_of(block, shape):
        count = count_ref[block]
        column_peer = lax.broadcasted_iota(jnp.int32, shape, 1) // TR
        live = jnp.zeros(shape, jnp.int32)
        for j in range(cands):
            slot = home_ref[cand_ref[block, j]] // (tile_count * count_mp)
            slot = jnp.where(j < count, slot, -1)
            live = jnp.where(column_peer == slot, 1, live)
        return live

    last_live[...] = live_of(blocks - 1, last_live.shape)

    def score(piece, live):
        mine = pl.ds(pl.multiple_of(piece[0], ALIGN), piece[1])
        raw = products(rows[mine, :], pool[:, pl.ds(0, width)])
        out_ref[mine, :] = profile_of(raw, pool, width, live, scale, logits)

    def score_unit(b, carry):
        score((b * UNIT, UNIT), live_of(b, (1, count_dp * TR)))
        return carry

    for b, piece in enumerate(pieces[:bulk]):
        rows_arrive(piece, b, near + far)
        first = piece[0] // UNIT
        lax.fori_loop(first, first + piece[1] // UNIT, score_unit, 0)
    b, piece = tail[-1]
    early_far = [(1 - side) * (half + 1) + i for i in range(half - 1)]
    rows_arrive(piece, b, near + early_far)
    last = pl.ds(*piece)
    same = pl.ds(pl.multiple_of(side * half * part, part), half * part)
    beyond = pl.ds(pl.multiple_of((1 - side) * (half + 1) * part, part), (half - 1) * part)
    last_rest[...] = products(rows[last, same], pool[:, same]) + products(rows[last, beyond], pool[:, beyond])
    for b, piece in tail[:-1]:
        rows_arrive(piece, b, near + far)
        score(piece, last_live[pl.ds(0, 1), :])
    b, piece = tail[-1]
    rows_arrive(piece, b, [opposite])

    for b, piece in enumerate(pieces):
        for target in near + far:
            send_rows(piece, b, target).wait_send()

    def finish_ids(i, carry):
        send_id(i).wait_send()
        return carry

    lax.fori_loop(1, count_dp, finish_ids, 0)

    def finish_tiles(i, carry):
        send_tile(i).wait_send()
        return carry

    lax.fori_loop(max(count_dp - slots, 1), count_dp, finish_tiles, 0)


def body(embeddings, centroids, labels, candidates, counts, home):
    count_dp = lax.axis_size("dp")
    count_mp = lax.axis_size("mp")
    part = embeddings.shape[1]
    width = centroids.shape[1]
    label_width = labels.shape[1]
    tile_count = centroids.shape[0] // TR
    blocks, cands = candidates.shape
    row_count = blocks * BR
    pieces = pieces_of(row_count)
    last_size = pieces[-1][1]
    both = width + label_width
    slots = count_dp - 1 if count_dp <= 8 else 3
    anywhere = pl.BlockSpec(memory_space=pl.ANY)
    local = pl.BlockSpec(memory_space=pltpu.VMEM)
    scale = 2.0 / math.sqrt(width)
    handed = [
        pltpu.VMEM((row_count - last_size, label_width), jnp.bfloat16),
        pltpu.VMEM((row_count, width), jnp.bfloat16),
        pltpu.VMEM((count_dp * TR, both), jnp.bfloat16),
        pltpu.VMEM((8, count_dp * TR), jnp.int32),
        pltpu.VMEM((last_size, count_dp * TR), jnp.float32),
    ]
    handed_bytes = 2 * ((row_count - last_size) * label_width + row_count * width) + count_dp * TR * (2 * both + 32 + 4 * last_size)
    held = pl.pallas_call(
        functools.partial(kernel, count_dp, count_mp, scale),
        in_specs=[anywhere] * 6,
        out_specs=[local] * len(handed),
        out_shape=handed,
        scratch_shapes=[
            pltpu.SMEM(candidates.shape, jnp.int32),
            pltpu.SMEM(counts.shape, jnp.int32),
            pltpu.SMEM(home.shape, jnp.int32),
            pltpu.VMEM((tile_count, TR, both), jnp.bfloat16),
            pltpu.VMEM((slots, TR, both), jnp.bfloat16),
            pltpu.VMEM((count_dp, 8, 128), jnp.int32),
            pltpu.VMEM((count_dp, 8, 128), jnp.int32),
            pltpu.VMEM((UNIT, count_dp * TR), jnp.float32),
            pltpu.SemaphoreType.DMA((count_mp, len(pieces))),
            pltpu.SemaphoreType.DMA((count_mp, len(pieces))),
            pltpu.SemaphoreType.DMA((count_dp,)),
            pltpu.SemaphoreType.DMA((count_dp,)),
            pltpu.SemaphoreType.REGULAR,
            pltpu.SemaphoreType.DMA((count_dp,)),
            pltpu.SemaphoreType.DMA((count_dp,)),
            pltpu.SemaphoreType.DMA((6,)),
        ],
        compiler_params=pltpu.CompilerParams(
            collective_id=0, has_side_effects=True, vmem_limit_bytes=VMEM_BYTES - handed_bytes
        ),
        name="annotate",
    )(
        candidates,
        counts,
        home,
        embeddings,
        centroids.reshape(tile_count, TR, width),
        labels.reshape(tile_count, TR, label_width),
    )
    return pl.pallas_call(
        functools.partial(close_kernel, count_mp, scale),
        in_specs=[local] * len(handed),
        out_specs=anywhere,
        out_shape=jax.ShapeDtypeStruct((row_count, label_width), jnp.bfloat16),
        scratch_shapes=[
            pltpu.VMEM((last_size, count_dp * TR), jnp.float32),
            pltpu.VMEM((last_size, label_width), jnp.bfloat16),
            pltpu.SemaphoreType.DMA((len(pieces),)),
        ],
        compiler_params=pltpu.CompilerParams(vmem_limit_bytes=CLOSE_BYTES),
        name="close",
    )(*[pltpu.with_memory_space_constraint(value, pltpu.VMEM) for value in held])


def solution(mesh):
    placed = (
        P("dp", "mp"),
        P(("dp", "mp"), None),
        P(("dp", "mp"), None),
        P(("dp", "mp"), None),
        P(("dp", "mp")),
        P(),
    )
    return jax.shard_map(
        body, mesh=mesh, in_specs=placed, out_specs=P(("dp", "mp"), None), check_vma=False
    )
```
